256 devices in a mesh: ma: 32 (over x, z), row: 8 (over y, core).
Axes of the slice: x: 4, y: 4, z: 8, core: 2. Of those that a mesh axis runs over, the one named last changes fastest.
Arguments:
- grid_field: bfloat16 [512, 1536, 512], P(None, 'ma', 'row'), may hold values from -6 to 6
- legendre: bfloat16 [512, 1024, 1536], P(('ma', 'row')), may hold values from -0.15625 to 0.15625
- order_table: int32 [512], P(('ma', 'row')), may hold values from 0 to 1023, as said below
- boundary_rows: int32 [2, 2], replicated, may hold values from 96 to 127, as said below
- inverse: bfloat16 [1024, 256, 256], P(('ma', 'row')), may hold values from -0.375 to 0.375
Outputs:
- spectra: bfloat16 [1024, 256, 1024], P(('ma', 'row'))
The draws below stay inside these ranges and needn't reach their ends.
Inputs may be any that keep to these rules, and one draw needn't show every extreme that they name: `order_table`: slots 2 i and 2 i + 1 hold the orders m and 1023 - m of one pair, m < 512 first; no order appears twice; the pair of 0 and 1023 is always present. `boundary_rows`: the four entries differ and lie in the top 128 // 4 Chebyshev rows; both ends of that range occur.
All inputs are finite; a program needn't handle non-finite values.
Results may differ from the reference program's by a relative error of at most 0.0049.
Values may be sent and summed in bfloat16 or wider, within the bound.
No kernel may reach another device: no remote copies, remote signals or barrier semaphores. Data moves between devices by JAX's collectives and lax.ppermute only.
A program may use at most 192 MiB of HBM per device.

```python
import jax
import jax.numpy as jnp
from jax import lax

L = 1024
NTHETA = 1536
NR = 128
M_WIN = 512


def draw_order_table(key, part):
    pair_count = M_WIN // 2
    first_key, second_key = jax.random.split(jax.random.fold_in(key, 11))
    others = jax.random.permutation(first_key, L // 2 - 1)[:pair_count - 1].astype(jnp.int32) + 1
    chosen = jnp.concatenate([jnp.zeros((1,), jnp.int32), others])
    chosen = jax.random.permutation(second_key, chosen).astype(jnp.int32)
    matched_pairs = jnp.stack([chosen, L - 1 - chosen], axis=1)
    return matched_pairs.reshape(M_WIN).astype(jnp.int32)


def draw_boundary_rows(key, part):
    quarter = NR // 4
    first_key, second_key = jax.random.split(jax.random.fold_in(key, 23))
    middle = jax.random.permutation(first_key, quarter - 2)[:2].astype(jnp.int32) + (NR - quarter + 1)
    ends = jnp.stack([jnp.full((), NR - 1, jnp.int32), jnp.full((), NR - quarter, jnp.int32)])
    values = jnp.concatenate([ends, middle])
    values = jax.random.permutation(second_key, values).astype(jnp.int32)
    return values.reshape(2, 2)


def block_scale(own_key, extent, cuts, low, largest):
    def one(position, shards_of):
        steps = jax.random.uniform(jax.random.fold_in(jax.random.fold_in(own_key, 6), position), (shards_of,), jnp.float32, low / len(cuts), largest / len(cuts))
        return jnp.repeat(jnp.exp(steps), extent[position] // shards_of).reshape((-1,) + (1,) * (len(extent) - position - 1))

    loudness = one(*cuts[0])
    for cut in cuts[1:]:
        loudness = loudness * one(*cut)
    return loudness


def centred(own_key, extent, spread, most, cuts=(), kind=jnp.bfloat16):
    entries = spread * jax.random.normal(own_key, extent, jnp.float32)
    if cuts:
        entries = entries * block_scale(own_key, extent, cuts, -0.22, 0.18)
    return jnp.clip(entries, -most, most).astype(kind)


def setup_inputs(seed: int = 0) -> dict:
    arg_keys = jax.random.split(jax.random.key(seed), 6)
    grid_field = centred(arg_keys[0], (M_WIN, NTHETA, 4 * NR), 1.0, 6.0, ((1, 32), (2, 8)))
    legendre = centred(arg_keys[1], (M_WIN, L, NTHETA), NTHETA ** -0.5, 0.15625, ((0, 256),))
    order_table = draw_order_table(jax.random.fold_in(arg_keys[5], 71), 0)
    boundary_rows = draw_boundary_rows(jax.random.fold_in(arg_keys[5], 71), 0)
    inverse = centred(arg_keys[4], (L, 2 * NR, 2 * NR), (2 * NR) ** -0.5, 0.375, ((0, 256),))
    return {"grid_field": grid_field, "legendre": legendre, "order_table": order_table, "boundary_rows": boundary_rows, "inverse": inverse}


def chebyshev_table(radial_levels):
    wave_number = jnp.arange(radial_levels, dtype=jnp.float32)[:, None]
    grid_point = jnp.arange(radial_levels, dtype=jnp.float32)[None, :]
    cos_table = jnp.cos(jnp.pi * wave_number * (grid_point + 0.5) / radial_levels) * jnp.sqrt(2.0 / radial_levels)
    return jnp.where(wave_number == 0.0, cos_table * jnp.sqrt(0.5), cos_table)

def boundary_keep(boundary_rows, radial_levels):
    row_index = jnp.arange(radial_levels, dtype=jnp.int32)[None, :]
    boundary_hit = (row_index == boundary_rows[:, 0:1]) | (row_index == boundary_rows[:, 1:2])
    return jnp.where(boundary_hit, 0.0, 1.0).astype(jnp.float32)

def reference(grid_field, legendre, order_table, boundary_rows, inverse):
    degrees = jnp.arange(L, dtype=jnp.int32)

    def one_slot(slot_items):
        table_rows, field_cols, order_value = slot_items
        matrix_product = jnp.dot(table_rows, field_cols, preferred_element_type=jnp.float32)
        return jnp.where((degrees >= order_value)[:, None], matrix_product, jnp.zeros_like(matrix_product))
    spectral_coefficients = lax.map(one_slot, (legendre, grid_field, order_table))
    spectral_coefficients = spectral_coefficients.reshape(M_WIN, L, NR, 2, 2)
    chebyshev = chebyshev_table(NR)
    coefficients = jnp.einsum('kj,sljqp->lqksp', chebyshev, spectral_coefficients, precision=lax.Precision.HIGHEST)
    keep_rows = boundary_keep(boundary_rows, NR)
    right_side = (coefficients * keep_rows[None, :, :, None, None]).reshape(L, 2 * NR, 2 * M_WIN)
    right_side = right_side.astype(jnp.bfloat16)

    def one_degree(degree_items):
        inverse_rows, right_rows = degree_items
        return jnp.dot(inverse_rows, right_rows, preferred_element_type=jnp.float32).astype(jnp.bfloat16)
    return lax.map(one_degree, (inverse, right_side))
```

```python
import jax
import jax.numpy as jnp
import ml_dtypes
import numpy as np
from jax import lax
from jax.experimental import pallas as pl
from jax.experimental.pallas import tpu as pltpu
from jax.sharding import PartitionSpec as P

AXES = ("ma", "row")
NR = 128
COLS = 4 * NR
LAT_STEP = 8
ROW_BLOCK = 256
SRC_STEP = 64
SRC_PERM = 32
VMEM = 56 * 1024 * 1024


def dot_nt(a, b):
    return lax.dot_general(a, b, (((1,), (1,)), ((), ())), preferred_element_type=jnp.float32)


def dot(a, b):
    return jnp.dot(a, b, preferred_element_type=jnp.float32)


def slot_unzip_matrix():
    m = np.zeros((256, 256), np.float32)
    for d in range(128):
        for h in range(2):
            m[2 * d + h, 128 * h + d] = 1.0
    return m.astype(ml_dtypes.bfloat16)


def chebyshev_matrices():
    k = np.arange(NR, dtype=np.float64)[:, None]
    j = np.arange(NR, dtype=np.float64)[None, :]
    table = np.cos(np.pi * k * (j + 0.5) / NR) * np.sqrt(2.0 / NR)
    table[0] = np.sqrt(1.0 / NR)
    full = np.zeros((COLS, COLS), np.float64)
    for p in range(2):
        for q in range(2):
            full[2 * q + p :: 4, 256 * p + 128 * q : 256 * p + 128 * q + 128] = table.T
    full = full.astype(np.float32)
    high = full.astype(ml_dtypes.bfloat16)
    low = (full - high.astype(np.float32)).astype(ml_dtypes.bfloat16)
    return high, low


def degree_gather_matrix():
    m = np.zeros((16 * SRC_PERM, 16 * SRC_PERM), np.float32)
    for p in range(2):
        for s in range(SRC_PERM):
            for h in range(2):
                for i in range(4):
                    m[((i * SRC_PERM + s) * 2 + h) * 2 + p, ((p * SRC_PERM + s) * 2 + h) * 4 + i] = 1.0
    return m.astype(ml_dtypes.bfloat16)


def pack_body(unzip_ref, x_ref, o_ref, f_ref):
    for g in range(2):
        x = x_ref[:, :, g * 256 : (g + 1) * 256].reshape(LAT_STEP * 64, 256)
        y = dot(x, unzip_ref[...])
        for t in range(LAT_STEP):
            rows = slice(t * 64, (t + 1) * 64)
            b = jnp.concatenate([y[rows, :128], y[rows, 128:]], axis=0)
            f_ref[pl.ds(g * 128 * LAT_STEP + t, 128, stride=LAT_STEP), :] = b.T
    o_ref[...] = f_ref[...].reshape(256, LAT_STEP, 128).astype(jnp.bfloat16)


def pack(grid_field):
    x = jnp.transpose(grid_field, (1, 2, 0))
    lat = x.shape[0]
    return pl.pallas_call(
        pack_body,
        name="pack",
        grid=(lat // LAT_STEP,),
        in_specs=[
            pl.BlockSpec((256, 256), lambda t: (0, 0)),
            pl.BlockSpec((LAT_STEP, 64, 512), lambda t: (t, 0, 0)),
        ],
        out_specs=pl.BlockSpec((256, LAT_STEP, 128), lambda t: (0, t, 0)),
        out_shape=jax.ShapeDtypeStruct((256, lat, 128), jnp.bfloat16),
        scratch_shapes=[pltpu.VMEM((256 * LAT_STEP, 128), jnp.float32)],
        compiler_params=pltpu.CompilerParams(vmem_limit_bytes=VMEM),
    )(jnp.asarray(slot_unzip_matrix()), x)


def analysis_body(order_ref, recv_ref, low_leg_ref, high_leg_ref, chi_ref, clo_ref, keep_ref, o_ref, f_ref):
    step = pl.program_id(0)

    @pl.when(step == 0)
    def _():
        lane = lax.broadcasted_iota(jnp.int32, (48, 128), 1)
        for a in range(32):
            for y in range(4):
                u = recv_ref[a * 8 + 2 * y]
                v = recv_ref[a * 8 + 2 * y + 1]
                ur = jnp.concatenate([u[:, 64:], u[:, :64]], axis=1)
                vr = jnp.concatenate([v[:, 64:], v[:, :64]], axis=1)
                f_ref[0, a * 48 : (a + 1) * 48, y * 128 : (y + 1) * 128] = jnp.where(lane < 64, u, vr)
                f_ref[1, a * 48 : (a + 1) * 48, y * 128 : (y + 1) * 128] = jnp.where(lane < 64, ur, v)

    degree = step * ROW_BLOCK + lax.broadcasted_iota(jnp.int32, (ROW_BLOCK, COLS), 0)

    def transform(leg, h):
        s = dot(leg, f_ref[h])
        s = jnp.where(degree >= order_ref[h], s, 0.0)
        hi = s.astype(jnp.bfloat16)
        lo = (s - hi.astype(jnp.float32)).astype(jnp.bfloat16)
        c = dot(hi, clo_ref[...]) + dot(lo, chi_ref[...]) + dot(hi, chi_ref[...])
        return (c * keep_ref[...]).reshape(ROW_BLOCK // 8, 8, COLS)

    sub = lax.broadcasted_iota(jnp.int32, (ROW_BLOCK // 8, 8, COLS), 1)

    def store(a, b):
        even = jnp.where(sub < 4, a, pltpu.roll(b, 4, 1))
        odd = jnp.where(sub < 4, pltpu.roll(a, 4, 1), b)
        both = jnp.stack([even, odd], axis=1).reshape(ROW_BLOCK // 4, 8, COLS)
        o_ref[...] = both.astype(jnp.bfloat16)

    @pl.when(step < 512 // ROW_BLOCK)
    def _():
        a = transform(low_leg_ref[0], 0)
        store(a, jnp.zeros_like(a))

    @pl.when(step >= 512 // ROW_BLOCK)
    def _():
        store(transform(low_leg_ref[0], 0), transform(high_leg_ref[0], 1))


def analysis(order_table, recv, legendre, keep):
    chi, clo = chebyshev_matrices()
    whole = lambda *shape: pl.BlockSpec(shape, lambda b: (0,) * len(shape))
    half = 512 // ROW_BLOCK
    return pl.pallas_call(
        analysis_body,
        name="analysis",
        grid=(1024 // ROW_BLOCK,),
        in_specs=[
            pl.BlockSpec(memory_space=pltpu.SMEM),
            whole(256, 48, 128),
            pl.BlockSpec((1, ROW_BLOCK, 1536), lambda b: (0, b, 0)),
            pl.BlockSpec((1, ROW_BLOCK, 1536), lambda b: (1, jnp.maximum(b, half), 0)),
            whole(COLS, COLS),
            whole(COLS, COLS),
            whole(1, COLS),
        ],
        out_specs=pl.BlockSpec((ROW_BLOCK // 4, 8, COLS), lambda b: (b, 0, 0)),
        out_shape=jax.ShapeDtypeStruct((256, 8, COLS), jnp.bfloat16),
        scratch_shapes=[pltpu.VMEM((2, 1536, COLS), jnp.bfloat16)],
        compiler_params=pltpu.CompilerParams(vmem_limit_bytes=VMEM),
    )(order_table, recv, legendre, legendre, jnp.asarray(chi), jnp.asarray(clo), keep)


def solve_body(gather_ref, recv_ref, inverse_ref, o_ref):
    parts = []
    for s in range(SRC_STEP // SRC_PERM):
        block = recv_ref[s * SRC_PERM : (s + 1) * SRC_PERM].reshape(SRC_PERM * 8, COLS)
        rows = jnp.concatenate([block[:, :256], block[:, 256:]], axis=0)
        parts.append(dot(gather_ref[...], rows).astype(jnp.bfloat16))
    per = 4 * SRC_PERM
    for i in range(4):
        r = jnp.concatenate([part[i * per : (i + 1) * per] for part in parts], axis=0)
        o_ref[i] = dot_nt(inverse_ref[i], r).astype(jnp.bfloat16)


def solve(recv, inverse):
    whole = lambda *shape: pl.BlockSpec(shape, lambda b: (0,) * len(shape))
    return pl.pallas_call(
        solve_body,
        name="solve",
        grid=(256 // SRC_STEP,),
        in_specs=[
            whole(16 * SRC_PERM, 16 * SRC_PERM),
            pl.BlockSpec((SRC_STEP, 8, COLS), lambda b: (b, 0, 0)),
            whole(4, 256, 256),
        ],
        out_specs=pl.BlockSpec((4, 256, 4 * SRC_STEP), lambda b: (0, 0, b)),
        out_shape=jax.ShapeDtypeStruct((4, 256, 1024), jnp.bfloat16),
        compiler_params=pltpu.CompilerParams(vmem_limit_bytes=VMEM),
    )(jnp.asarray(degree_gather_matrix()), recv, inverse)


def keep_columns(boundary_rows):
    k = jnp.arange(NR, dtype=jnp.int32)[None, :]
    hit = (k == boundary_rows[:, 0:1]) | (k == boundary_rows[:, 1:2])
    keep = jnp.where(hit, 0.0, 1.0).astype(jnp.float32).reshape(1, 2 * NR)
    return jnp.concatenate([keep, keep], axis=1)


def exchange(x):
    return lax.all_to_all(x, AXES, split_axis=0, concat_axis=0, tiled=True)


def on_device(grid_field, legendre, order_table, boundary_rows, inverse):
    keep = keep_columns(boundary_rows)
    field = exchange(pack(grid_field))
    right_side = exchange(analysis(order_table, field, legendre, keep))
    return solve(right_side, inverse)


def solution(mesh):
    return jax.shard_map(
        on_device,
        mesh=mesh,
        in_specs=(
            P(None, "ma", "row"),
            P(("ma", "row"), None, None),
            P(("ma", "row")),
            P(),
            P(("ma", "row"), None, None),
        ),
        out_specs=P(("ma", "row"), None, None),
        check_vma=False,
    )
```

```python
import jax
import jax.numpy as jnp
import ml_dtypes
import numpy as np
from jax import lax
from jax.experimental import pallas as pl
from jax.experimental.pallas import tpu as pltpu
from jax.sharding import PartitionSpec as P

AXES = ("ma", "row")
NR = 128
COLS = 4 * NR
LAT_STEP = 24
ROW_BLOCK = 256
SRC_STEP = 64
SRC_PERM = 32
MIB = 1024 * 1024


def dot_nt(a, b):
    return lax.dot_general(a, b, (((1,), (1,)), ((), ())), preferred_element_type=jnp.float32)


def dot(a, b):
    return jnp.dot(a, b, preferred_element_type=jnp.float32)


def chebyshev_matrices():
    k = np.arange(NR, dtype=np.float64)[:, None]
    j = np.arange(NR, dtype=np.float64)[None, :]
    table = np.cos(np.pi * k * (j + 0.5) / NR) * np.sqrt(2.0 / NR)
    table[0] = np.sqrt(1.0 / NR)
    full = np.zeros((COLS, COLS), np.float64)
    for p in range(2):
        for q in range(2):
            full[2 * q + p :: 4, 256 * p + 128 * q : 256 * p + 128 * q + 128] = table.T
    full = full.astype(np.float32)
    swapped = full.reshape(4, 2, 64, COLS)[:, ::-1].reshape(COLS, COLS)
    full = np.stack([full, swapped])
    high = full.astype(ml_dtypes.bfloat16)
    low = (full - high.astype(np.float32)).astype(ml_dtypes.bfloat16)
    return high, low


def degree_gather_matrix():
    m = np.zeros((16 * SRC_PERM, 16 * SRC_PERM), np.float32)
    for p in range(2):
        for s in range(SRC_PERM):
            for h in range(2):
                for i in range(4):
                    m[((i * SRC_PERM + s) * 2 + h) * 2 + p, ((p * SRC_PERM + s) * 2 + h) * 4 + i] = 1.0
    return m.astype(ml_dtypes.bfloat16)


def pack_body(core_ref, x_hbm, o_hbm, x_ref, f_ref, o_ref, in_sem, out_sem):
    chunks = x_hbm.shape[0] // LAT_STEP

    def fetch(i):
        part = pl.ds(i * LAT_STEP, LAT_STEP)
        return pltpu.make_async_copy(x_hbm.at[part], x_ref.at[part], in_sem.at[i])

    def flush(i):
        part = pl.ds(i * LAT_STEP, LAT_STEP)
        return pltpu.make_async_copy(o_ref.at[:, part, :], o_hbm.at[:, part, :], out_sem.at[i])

    for i in range(chunks):
        fetch(i).start()
    source = lax.broadcasted_iota(jnp.int32, (256, 256), 0)
    target = lax.broadcasted_iota(jnp.int32, (256, 256), 1)
    first = source == 2 * (target % 128) + target // 128
    second = source == 2 * (target % 128) + 1 - target // 128
    unzip = jnp.where(core_ref[0] == 0, first.astype(jnp.float32), second.astype(jnp.float32)).astype(jnp.bfloat16)
    for i in range(chunks):
        fetch(i).wait()
        for g in range(2):
            x = x_ref[i * LAT_STEP : (i + 1) * LAT_STEP, :, g * 256 : (g + 1) * 256]
            y = dot(x.reshape(LAT_STEP * 64, 256), unzip).astype(jnp.bfloat16)
            for t in range(LAT_STEP):
                rows = slice(t * 64, (t + 1) * 64)
                b = jnp.concatenate([y[rows, :128], y[rows, 128:]], axis=0)
                f_ref[i, pl.ds(g * 128 * LAT_STEP + t, 128, stride=LAT_STEP), :] = b.T.astype(jnp.float32)
        o_ref[:, i * LAT_STEP : (i + 1) * LAT_STEP, :] = f_ref[i].reshape(256, LAT_STEP, 128).astype(jnp.bfloat16)
        flush(i).start()
    for i in range(chunks):
        flush(i).wait()


def pack(grid_field, core):
    x = jnp.transpose(grid_field, (1, 2, 0))
    lat = x.shape[0]
    chunks = lat // LAT_STEP
    return pl.pallas_call(
        pack_body,
        name="pack",
        in_specs=[pl.BlockSpec(memory_space=pltpu.SMEM), pl.BlockSpec(memory_space=pltpu.HBM)],
        out_specs=pl.BlockSpec(memory_space=pltpu.HBM),
        out_shape=jax.ShapeDtypeStruct((256, lat, 128), jnp.bfloat16),
        scratch_shapes=[
            pltpu.VMEM(x.shape, jnp.bfloat16),
            pltpu.VMEM((chunks, 256 * LAT_STEP, 128), jnp.float32),
            pltpu.VMEM((256, lat, 128), jnp.bfloat16),
            pltpu.SemaphoreType.DMA((chunks,)),
            pltpu.SemaphoreType.DMA((chunks,)),
        ],
        compiler_params=pltpu.CompilerParams(vmem_limit_bytes=58 * MIB),
    )(core, x)


def analysis_body(order_ref, boundary_ref, recv_ref, leg_ref, chi_ref, clo_ref, o_ref, f_ref):
    column = lax.broadcasted_iota(jnp.int32, (1, COLS), 1)
    mode, second = column % NR, (column // NR) % 2 == 1
    keep = jnp.ones((1, COLS), jnp.float32)
    for e in range(2):
        keep = jnp.where(mode == jnp.where(second, boundary_ref[1, e], boundary_ref[0, e]), 0.0, keep)
    lane = lax.broadcasted_iota(jnp.int32, (48, 128), 1)
    for a in range(32):
        for y in range(4):
            u = recv_ref[a * 8 + 2 * y]
            v = recv_ref[a * 8 + 2 * y + 1]
            f_ref[0, a * 48 : (a + 1) * 48, y * 128 : (y + 1) * 128] = jnp.where(lane < 64, u, v)
            f_ref[1, a * 48 : (a + 1) * 48, y * 128 : (y + 1) * 128] = jnp.where(lane < 64, v, u)

    iota = lax.broadcasted_iota(jnp.int32, (ROW_BLOCK, COLS), 0)
    sub = lax.broadcasted_iota(jnp.int32, (ROW_BLOCK // 8, 8, COLS), 1)
    step = ROW_BLOCK // 4

    def transform(h, block):
        s = dot(leg_ref[h, block * ROW_BLOCK : (block + 1) * ROW_BLOCK], f_ref[h])
        s = jnp.where(iota + block * ROW_BLOCK >= order_ref[h], s, 0.0)
        hi = s.astype(jnp.bfloat16)
        lo = (s - hi.astype(jnp.float32)).astype(jnp.bfloat16)
        c = dot(hi, clo_ref[h]) + dot(lo, chi_ref[h]) + dot(hi, chi_ref[h])
        return (c * keep).reshape(ROW_BLOCK // 8, 8, COLS)

    def store(block, a, b):
        if b is None:
            even = jnp.where(sub < 4, a, 0.0)
            odd = jnp.where(sub < 4, pltpu.roll(a, 4, 1), 0.0)
        else:
            even = jnp.where(sub < 4, a, pltpu.roll(b, 4, 1))
            odd = jnp.where(sub < 4, pltpu.roll(a, 4, 1), b)
        both = jnp.stack([even, odd], axis=1).reshape(step, 8, COLS)
        o_ref[block * step : (block + 1) * step] = both.astype(jnp.bfloat16)

    for block in range(1024 // ROW_BLOCK):
        low, high = block * ROW_BLOCK, (block + 1) * ROW_BLOCK
        even_on = order_ref[0] < high
        odd_on = order_ref[1] < high

        @pl.when(jnp.logical_not(even_on))
        def _():
            o_ref[block * step : (block + 1) * step] = jnp.zeros((step, 8, COLS), jnp.bfloat16)

        @pl.when(jnp.logical_and(even_on, jnp.logical_not(odd_on)))
        def _():
            store(block, transform(0, block), None)

        if high > 512:

            @pl.when(odd_on)
            def _():
                store(block, transform(0, block), transform(1, block))


def analysis(order_table, boundary_rows, recv, legendre):
    chi, clo = chebyshev_matrices()
    smem = pl.BlockSpec(memory_space=pltpu.SMEM)
    vmem = pl.BlockSpec(memory_space=pltpu.VMEM)
    return pl.pallas_call(
        analysis_body,
        name="analysis",
        in_specs=[smem, smem, vmem, vmem, vmem, vmem],
        out_specs=vmem,
        out_shape=jax.ShapeDtypeStruct((256, 8, COLS), jnp.bfloat16),
        scratch_shapes=[pltpu.VMEM((2, 1536, COLS), jnp.bfloat16)],
        compiler_params=pltpu.CompilerParams(vmem_limit_bytes=24 * MIB),
    )(order_table, boundary_rows, recv, legendre, jnp.asarray(chi), jnp.asarray(clo))


def solve_body(gather_ref, recv_ref, inverse_ref, o_ref):
    parts = []
    first = pl.program_id(0) * SRC_STEP
    for s in range(SRC_STEP // SRC_PERM):
        block = recv_ref[pl.ds(first + s * SRC_PERM, SRC_PERM)].reshape(SRC_PERM * 8, COLS)
        rows = jnp.concatenate([block[:, :256], block[:, 256:]], axis=0)
        parts.append(dot(gather_ref[...], rows).astype(jnp.bfloat16))
    per = 4 * SRC_PERM
    for i in range(4):
        r = jnp.concatenate([part[i * per : (i + 1) * per] for part in parts], axis=0)
        o_ref[i] = dot_nt(inverse_ref[i], r).astype(jnp.bfloat16)


def solve(recv, inverse):
    vmem = pl.BlockSpec(memory_space=pltpu.VMEM)
    return pl.pallas_call(
        solve_body,
        name="solve",
        grid=(256 // SRC_STEP,),
        in_specs=[
            vmem,
            vmem,
            vmem,
        ],
        out_specs=pl.BlockSpec((4, 256, 4 * SRC_STEP), lambda b: (0, 0, b)),
        out_shape=jax.ShapeDtypeStruct((4, 256, 1024), jnp.bfloat16),
        compiler_params=pltpu.CompilerParams(vmem_limit_bytes=16 * MIB),
    )(jnp.asarray(degree_gather_matrix()), recv, inverse)


def exchange(x):
    return lax.all_to_all(x, AXES, split_axis=0, concat_axis=0, tiled=True)


def on_device(grid_field, legendre, order_table, boundary_rows, inverse):
    core = (lax.axis_index("row") % 2).astype(jnp.int32).reshape(1)
    field = exchange(pack(grid_field, core))
    right_side = exchange(analysis(order_table, boundary_rows, field, legendre))
    return solve(right_side, inverse)


def solution(mesh):
    return jax.shard_map(
        on_device,
        mesh=mesh,
        in_specs=(
            P(None, "ma", "row"),
            P(("ma", "row"), None, None),
            P(("ma", "row")),
            P(),
            P(("ma", "row"), None, None),
        ),
        out_specs=P(("ma", "row"), None, None),
        check_vma=False,
    )
```

```python
import jax
import jax.numpy as jnp
import ml_dtypes
import numpy as np
from jax import lax
from jax.experimental import pallas as pl
from jax.experimental.pallas import tpu as pltpu
from jax.sharding import PartitionSpec as P

AXES = ("ma", "row")
NR = 128
COLS = 4 * NR
LAT_STEP = 24
ROW_BLOCK = 256
SRC_STEP = 128
SRC_PERM = 16
MIB = 1024 * 1024


def dot_nt(a, b):
    return lax.dot_general(a, b, (((1,), (1,)), ((), ())), preferred_element_type=jnp.float32)


def dot(a, b):
    return jnp.dot(a, b, preferred_element_type=jnp.float32)


def chebyshev_matrices():
    k = np.arange(NR, dtype=np.float64)[:, None]
    j = np.arange(NR, dtype=np.float64)[None, :]
    table = np.cos(np.pi * k * (j + 0.5) / NR) * np.sqrt(2.0 / NR)
    table[0] = np.sqrt(1.0 / NR)
    full = np.zeros((COLS, COLS), np.float64)
    for p in range(2):
        for q in range(2):
            full[2 * q + p :: 4, 256 * p + 128 * q : 256 * p + 128 * q + 128] = table.T
    full = full.astype(np.float32)
    swapped = full.reshape(4, 2, 64, COLS)[:, ::-1].reshape(COLS, COLS)
    full = np.stack([full, swapped])
    high = full.astype(ml_dtypes.bfloat16)
    low = (full - high.astype(np.float32)).astype(ml_dtypes.bfloat16)
    return high, low


def degree_gather_matrix():
    m = np.zeros((16 * SRC_PERM, 16 * SRC_PERM), np.float32)
    for p in range(2):
        for s in range(SRC_PERM):
            for h in range(2):
                for i in range(4):
                    m[((i * SRC_PERM + s) * 2 + h) * 2 + p, ((p * SRC_PERM + s) * 2 + h) * 4 + i] = 1.0
    return m.astype(ml_dtypes.bfloat16)


def pack_body(core_ref, x_hbm, o_hbm, x_ref, f_ref, o_ref, in_sem, out_sem):
    chunks = x_hbm.shape[0] // LAT_STEP

    def fetch(i):
        part = pl.ds(i * LAT_STEP, LAT_STEP)
        return pltpu.make_async_copy(x_hbm.at[part], x_ref.at[part], in_sem.at[i])

    def flush(i):
        part = pl.ds(i * LAT_STEP, LAT_STEP)
        return pltpu.make_async_copy(o_ref.at[:, part, :], o_hbm.at[:, part, :], out_sem.at[i])

    for i in range(chunks):
        fetch(i).start()
    source = lax.broadcasted_iota(jnp.int32, (256, 256), 0)
    target = lax.broadcasted_iota(jnp.int32, (256, 256), 1)
    first = source == 2 * (target % 128) + target // 128
    second = source == 2 * (target % 128) + 1 - target // 128
    unzip = jnp.where(core_ref[0] == 0, first.astype(jnp.float32), second.astype(jnp.float32)).astype(jnp.bfloat16)
    for i in range(chunks):
        fetch(i).wait()
        for g in range(2):
            x = x_ref[i * LAT_STEP : (i + 1) * LAT_STEP, :, g * 256 : (g + 1) * 256]
            y = dot(x.reshape(LAT_STEP * 64, 256), unzip).astype(jnp.bfloat16)
            for t in range(LAT_STEP):
                rows = slice(t * 64, (t + 1) * 64)
                b = jnp.concatenate([y[rows, :128], y[rows, 128:]], axis=0)
                f_ref[i, pl.ds(g * 128 * LAT_STEP + t, 128, stride=LAT_STEP), :] = b.T.astype(jnp.float32)
        o_ref[:, i * LAT_STEP : (i + 1) * LAT_STEP, :] = f_ref[i].reshape(256, LAT_STEP, 128).astype(jnp.bfloat16)
        flush(i).start()
    for i in range(chunks):
        flush(i).wait()


def pack(grid_field, core):
    x = jnp.transpose(grid_field, (1, 2, 0))
    lat = x.shape[0]
    chunks = lat // LAT_STEP
    return pl.pallas_call(
        pack_body,
        name="pack",
        in_specs=[pl.BlockSpec(memory_space=pltpu.SMEM), pl.BlockSpec(memory_space=pltpu.HBM)],
        out_specs=pl.BlockSpec(memory_space=pltpu.HBM),
        out_shape=jax.ShapeDtypeStruct((256, lat, 128), jnp.bfloat16),
        scratch_shapes=[
            pltpu.VMEM(x.shape, jnp.bfloat16),
            pltpu.VMEM((chunks, 256 * LAT_STEP, 128), jnp.float32),
            pltpu.VMEM((256, lat, 128), jnp.bfloat16),
            pltpu.SemaphoreType.DMA((chunks,)),
            pltpu.SemaphoreType.DMA((chunks,)),
        ],
        compiler_params=pltpu.CompilerParams(vmem_limit_bytes=58 * MIB),
    )(core, x)


def analysis_body(order_ref, boundary_ref, recv_ref, leg_ref, chi_ref, clo_ref, o_ref, f_ref):
    column = lax.broadcasted_iota(jnp.int32, (1, COLS), 1)
    mode, second = column % NR, (column // NR) % 2 == 1
    keep = jnp.ones((1, COLS), jnp.float32)
    for e in range(2):
        keep = jnp.where(mode == jnp.where(second, boundary_ref[1, e], boundary_ref[0, e]), 0.0, keep)
    lane = lax.broadcasted_iota(jnp.int32, (48, 128), 1)
    for a in range(32):
        for y in range(4):
            u = recv_ref[a * 8 + 2 * y]
            v = recv_ref[a * 8 + 2 * y + 1]
            f_ref[0, a * 48 : (a + 1) * 48, y * 128 : (y + 1) * 128] = jnp.where(lane < 64, u, v)
            f_ref[1, a * 48 : (a + 1) * 48, y * 128 : (y + 1) * 128] = jnp.where(lane < 64, v, u)

    iota = lax.broadcasted_iota(jnp.int32, (ROW_BLOCK, COLS), 0)
    sub = lax.broadcasted_iota(jnp.int32, (ROW_BLOCK // 8, 8, COLS), 1)
    step = ROW_BLOCK // 4

    def spectrum(h, block, masked):
        first = block * ROW_BLOCK
        if not isinstance(block, int):
            first = pl.multiple_of(first, ROW_BLOCK)
        s = dot(leg_ref[h, pl.ds(first, ROW_BLOCK)], f_ref[h])
        return jnp.where(iota + first >= order_ref[h], s, 0.0) if masked else s

    def transform(h, s):
        hi = s.astype(jnp.bfloat16)
        lo = (s - hi.astype(jnp.float32)).astype(jnp.bfloat16)
        c = dot(hi, clo_ref[h]) + dot(lo, chi_ref[h]) + dot(hi, chi_ref[h])
        return (c * keep).reshape(ROW_BLOCK // 8, 8, COLS)

    def store(block, a, b):
        even = jnp.where(sub < 4, a, 0.0 if b is None else pltpu.roll(b, 4, 1))
        odd = jnp.where(sub < 4, pltpu.roll(a, 4, 1), 0.0 if b is None else b)
        both = jnp.stack([even, odd], axis=1).reshape(step, 8, COLS)
        o_ref[block * step : (block + 1) * step] = both.astype(jnp.bfloat16)

    low_order = order_ref[0] < ROW_BLOCK
    h = jnp.where(low_order, 0, 1)
    s0 = spectrum(h, jnp.where(low_order, 0, 2), True)
    s1 = spectrum(0, 1, True)
    either = transform(h, s0)
    s2 = spectrum(0, 2, False)
    store(0, jnp.where(low_order, either, 0.0), None)
    c1 = transform(0, s1)
    s3 = spectrum(0, 3, False)
    store(1, c1, None)
    c2 = transform(0, s2)
    s4 = spectrum(1, 3, True)
    store(2, c2, jnp.where(low_order, 0.0, either))
    c3 = transform(0, s3)
    c4 = transform(1, s4)
    store(3, c3, c4)


def analysis(order_table, boundary_rows, recv, legendre):
    chi, clo = chebyshev_matrices()
    smem = pl.BlockSpec(memory_space=pltpu.SMEM)
    vmem = pl.BlockSpec(memory_space=pltpu.VMEM)
    return pl.pallas_call(
        analysis_body,
        name="analysis",
        in_specs=[smem, smem, vmem, vmem, vmem, vmem],
        out_specs=vmem,
        out_shape=jax.ShapeDtypeStruct((256, 8, COLS), jnp.bfloat16),
        scratch_shapes=[pltpu.VMEM((2, 1536, COLS), jnp.bfloat16)],
        compiler_params=pltpu.CompilerParams(vmem_limit_bytes=24 * MIB),
    )(order_table, boundary_rows, recv, legendre, jnp.asarray(chi), jnp.asarray(clo))


def solve_body(gather_ref, recv_ref, inverse_ref, o_hbm, o_ref, sem):
    chunks = 256 // SRC_STEP
    wide = 4 * SRC_STEP

    def flush(c):
        part = pl.ds(c * wide, wide)
        return pltpu.make_async_copy(o_ref.at[:, :, part], o_hbm.at[:, :, part], sem.at[c])

    per = 4 * SRC_PERM
    for c in range(chunks):
        parts = []
        for first in range(c * SRC_STEP, (c + 1) * SRC_STEP, SRC_PERM):
            block = recv_ref[first : first + SRC_PERM].reshape(SRC_PERM * 8, COLS)
            rows = jnp.concatenate([block[:, :256], block[:, 256:]], axis=0)
            parts.append(dot(gather_ref[...], rows).astype(jnp.bfloat16))
        for i in range(4):
            r = jnp.concatenate([part[i * per : (i + 1) * per] for part in parts], axis=0)
            o_ref[i, :, c * wide : (c + 1) * wide] = dot_nt(inverse_ref[i], r).astype(jnp.bfloat16)
        flush(c).start()
    for c in range(chunks):
        flush(c).wait()


def solve(recv, inverse):
    vmem = pl.BlockSpec(memory_space=pltpu.VMEM)
    return pl.pallas_call(
        solve_body,
        name="solve",
        in_specs=[vmem, vmem, vmem],
        out_specs=pl.BlockSpec(memory_space=pltpu.HBM),
        out_shape=jax.ShapeDtypeStruct((4, 256, 1024), jnp.bfloat16),
        scratch_shapes=[
            pltpu.VMEM((4, 256, 1024), jnp.bfloat16),
            pltpu.SemaphoreType.DMA((256 // SRC_STEP,)),
        ],
        compiler_params=pltpu.CompilerParams(vmem_limit_bytes=16 * MIB),
    )(jnp.asarray(degree_gather_matrix()), recv, inverse)


def exchange(x):
    return lax.all_to_all(x, AXES, split_axis=0, concat_axis=0, tiled=True)


def on_device(grid_field, legendre, order_table, boundary_rows, inverse):
    core = (lax.axis_index("row") % 2).astype(jnp.int32).reshape(1)
    field = exchange(pack(grid_field, core))
    right_side = exchange(analysis(order_table, boundary_rows, field, legendre))
    return solve(right_side, inverse)


def solution(mesh):
    return jax.shard_map(
        on_device,
        mesh=mesh,
        in_specs=(
            P(None, "ma", "row"),
            P(("ma", "row"), None, None),
            P(("ma", "row")),
            P(),
            P(("ma", "row"), None, None),
        ),
        out_specs=P(("ma", "row"), None, None),
        check_vma=False,
    )
```

```python
import jax
import jax.numpy as jnp
import ml_dtypes
import numpy as np
from jax import lax
from jax.experimental import pallas as pl
from jax.experimental.pallas import tpu as pltpu
from jax.sharding import PartitionSpec as P

AXES = ("ma", "row")
NR = 128
COLS = 4 * NR
LAT_CHUNKS = (16, 24, 8)
LAT_PITCH = 24
ROW_BLOCK = 256
SRC_STEP = 128
SRC_PERM = 16
MIB = 1024 * 1024


def dot_nt(a, b):
    return lax.dot_general(a, b, (((1,), (1,)), ((), ())), preferred_element_type=jnp.float32)


def dot(a, b):
    return jnp.dot(a, b, preferred_element_type=jnp.float32)


def chebyshev_matrices():
    k = np.arange(NR, dtype=np.float64)[:, None]
    j = np.arange(NR, dtype=np.float64)[None, :]
    table = np.cos(np.pi * k * (j + 0.5) / NR) * np.sqrt(2.0 / NR)
    table[0] = np.sqrt(1.0 / NR)
    full = np.zeros((COLS, COLS), np.float64)
    for p in range(2):
        for q in range(2):
            full[2 * q + p :: 4, 256 * p + 128 * q : 256 * p + 128 * q + 128] = table.T
    full = full.astype(np.float32)
    swapped = full.reshape(4, 2, 64, COLS)[:, ::-1].reshape(COLS, COLS)
    full = np.stack([full, swapped])
    high = full.astype(ml_dtypes.bfloat16)
    low = (full - high.astype(np.float32)).astype(ml_dtypes.bfloat16)
    return high, low


def degree_gather_matrix():
    m = np.zeros((16 * SRC_PERM, 16 * SRC_PERM), np.float32)
    for p in range(2):
        for s in range(SRC_PERM):
            for h in range(2):
                for i in range(4):
                    m[((i * SRC_PERM + s) * 2 + h) * 2 + p, ((p * SRC_PERM + s) * 2 + h) * 4 + i] = 1.0
    return m.astype(ml_dtypes.bfloat16)


def pack_body(core_ref, x_hbm, o_hbm, x_ref, f_ref, o_ref, in_sem, out_sem):
    starts = [sum(LAT_CHUNKS[:i]) for i in range(len(LAT_CHUNKS))]
    parts = [pl.ds(first, size) for first, size in zip(starts, LAT_CHUNKS)]

    def fetch(i):
        return pltpu.make_async_copy(x_hbm.at[parts[i]], x_ref.at[parts[i]], in_sem.at[i])

    def flush(i):
        return pltpu.make_async_copy(o_ref.at[:, parts[i], :], o_hbm.at[:, parts[i], :], out_sem.at[i])

    for i in range(len(parts)):
        fetch(i).start()
    source = lax.broadcasted_iota(jnp.int32, (256, 256), 0)
    target = lax.broadcasted_iota(jnp.int32, (256, 256), 1)
    first = source == 2 * (target % 128) + target // 128
    second = source == 2 * (target % 128) + 1 - target // 128
    unzip = jnp.where(core_ref[0] == 0, first.astype(jnp.float32), second.astype(jnp.float32)).astype(jnp.bfloat16)
    for i, (start, size) in enumerate(zip(starts, LAT_CHUNKS)):
        lat = slice(start, start + size)
        fetch(i).wait()
        for g in range(2):
            x = x_ref[lat, :, g * 256 : (g + 1) * 256].reshape(size * 64, 256)
            y = dot(x, unzip).astype(jnp.bfloat16)
            for t in range(size):
                rows = slice(t * 64, (t + 1) * 64)
                b = jnp.concatenate([y[rows, :128], y[rows, 128:]], axis=0)
                f_ref[i, pl.ds(g * 128 * LAT_PITCH + t, 128, stride=LAT_PITCH), :] = b.T.astype(jnp.float32)
        o_ref[:, lat, :] = f_ref[i].reshape(256, LAT_PITCH, 128)[:, :size].astype(jnp.bfloat16)
        flush(i).start()
    for i in range(len(parts)):
        flush(i).wait()


def pack(grid_field, core):
    x = jnp.transpose(grid_field, (1, 2, 0))
    lat = x.shape[0]
    chunks = len(LAT_CHUNKS)
    return pl.pallas_call(
        pack_body,
        name="pack",
        in_specs=[pl.BlockSpec(memory_space=pltpu.SMEM), pl.BlockSpec(memory_space=pltpu.HBM)],
        out_specs=pl.BlockSpec(memory_space=pltpu.HBM),
        out_shape=jax.ShapeDtypeStruct((256, lat, 128), jnp.bfloat16),
        scratch_shapes=[
            pltpu.VMEM(x.shape, jnp.bfloat16),
            pltpu.VMEM((chunks, 256 * LAT_PITCH, 128), jnp.float32),
            pltpu.VMEM((256, lat, 128), jnp.bfloat16),
            pltpu.SemaphoreType.DMA((chunks,)),
            pltpu.SemaphoreType.DMA((chunks,)),
        ],
        compiler_params=pltpu.CompilerParams(vmem_limit_bytes=58 * MIB),
    )(core, x)


def analysis_body(order_ref, boundary_ref, recv_ref, leg_ref, chi_ref, clo_ref, o_ref, f_ref):
    column = lax.broadcasted_iota(jnp.int32, (1, COLS), 1)
    mode, second = column % NR, (column // NR) % 2 == 1
    keep = jnp.ones((1, COLS), jnp.float32)
    for e in range(2):
        keep = jnp.where(mode == jnp.where(second, boundary_ref[1, e], boundary_ref[0, e]), 0.0, keep)
    lane = lax.broadcasted_iota(jnp.int32, (48, 128), 1)
    for a in range(32):
        for y in range(4):
            u = recv_ref[a * 8 + 2 * y]
            v = recv_ref[a * 8 + 2 * y + 1]
            f_ref[0, a * 48 : (a + 1) * 48, y * 128 : (y + 1) * 128] = jnp.where(lane < 64, u, v)
            f_ref[1, a * 48 : (a + 1) * 48, y * 128 : (y + 1) * 128] = jnp.where(lane < 64, v, u)

    iota = lax.broadcasted_iota(jnp.int32, (ROW_BLOCK, COLS), 0)
    sub = lax.broadcasted_iota(jnp.int32, (ROW_BLOCK // 8, 8, COLS), 1)
    step = ROW_BLOCK // 4

    def spectrum(h, block, masked):
        first = block * ROW_BLOCK
        if not isinstance(block, int):
            first = pl.multiple_of(first, ROW_BLOCK)
        s = dot(leg_ref[h, pl.ds(first, ROW_BLOCK)], f_ref[h])
        return jnp.where(iota + first >= order_ref[h], s, 0.0) if masked else s

    def transform(h, s):
        hi = s.astype(jnp.bfloat16)
        lo = (s - hi.astype(jnp.float32)).astype(jnp.bfloat16)
        c = dot(hi, clo_ref[h]) + dot(lo, chi_ref[h]) + dot(hi, chi_ref[h])
        return (c * keep).reshape(ROW_BLOCK // 8, 8, COLS)

    def store(block, a, b):
        even = jnp.where(sub < 4, a, 0.0 if b is None else pltpu.roll(b, 4, 1))
        odd = jnp.where(sub < 4, pltpu.roll(a, 4, 1), 0.0 if b is None else b)
        both = jnp.stack([even, odd], axis=1).reshape(step, 8, COLS)
        o_ref[block * step : (block + 1) * step] = both.astype(jnp.bfloat16)

    low_order = order_ref[0] < ROW_BLOCK
    h = jnp.where(low_order, 0, 1)
    s0 = spectrum(h, jnp.where(low_order, 0, 2), True)
    s1 = spectrum(0, 1, True)
    either = transform(h, s0)
    s2 = spectrum(0, 2, False)
    store(0, jnp.where(low_order, either, 0.0), None)
    c1 = transform(0, s1)
    s3 = spectrum(0, 3, False)
    store(1, c1, None)
    c2 = transform(0, s2)
    s4 = spectrum(1, 3, True)
    store(2, c2, jnp.where(low_order, 0.0, either))
    c3 = transform(0, s3)
    c4 = transform(1, s4)
    store(3, c3, c4)


def analysis(order_table, boundary_rows, recv, legendre):
    chi, clo = chebyshev_matrices()
    smem = pl.BlockSpec(memory_space=pltpu.SMEM)
    vmem = pl.BlockSpec(memory_space=pltpu.VMEM)
    return pl.pallas_call(
        analysis_body,
        name="analysis",
        in_specs=[smem, smem, vmem, vmem, vmem, vmem],
        out_specs=vmem,
        out_shape=jax.ShapeDtypeStruct((256, 8, COLS), jnp.bfloat16),
        scratch_shapes=[pltpu.VMEM((2, 1536, COLS), jnp.bfloat16)],
        compiler_params=pltpu.CompilerParams(vmem_limit_bytes=24 * MIB),
    )(order_table, boundary_rows, recv, legendre, jnp.asarray(chi), jnp.asarray(clo))


def solve_body(gather_ref, recv_ref, inverse_ref, o_hbm, o_ref, sem):
    chunks = 256 // SRC_STEP
    wide = 4 * SRC_STEP

    def flush(c):
        part = pl.ds(c * wide, wide)
        return pltpu.make_async_copy(o_ref.at[:, :, part], o_hbm.at[:, :, part], sem.at[c])

    per = 4 * SRC_PERM
    for c in range(chunks):
        parts = []
        for first in range(c * SRC_STEP, (c + 1) * SRC_STEP, SRC_PERM):
            block = recv_ref[first : first + SRC_PERM].reshape(SRC_PERM * 8, COLS)
            rows = jnp.concatenate([block[:, :256], block[:, 256:]], axis=0)
            parts.append(dot(gather_ref[...], rows).astype(jnp.bfloat16))
        for i in range(4):
            r = jnp.concatenate([part[i * per : (i + 1) * per] for part in parts], axis=0)
            o_ref[i, :, c * wide : (c + 1) * wide] = dot_nt(inverse_ref[i], r).astype(jnp.bfloat16)
        flush(c).start()
    for c in range(chunks):
        flush(c).wait()


def solve(recv, inverse):
    vmem = pl.BlockSpec(memory_space=pltpu.VMEM)
    return pl.pallas_call(
        solve_body,
        name="solve",
        in_specs=[vmem, vmem, vmem],
        out_specs=pl.BlockSpec(memory_space=pltpu.HBM),
        out_shape=jax.ShapeDtypeStruct((4, 256, 1024), jnp.bfloat16),
        scratch_shapes=[
            pltpu.VMEM((4, 256, 1024), jnp.bfloat16),
            pltpu.SemaphoreType.DMA((256 // SRC_STEP,)),
        ],
        compiler_params=pltpu.CompilerParams(vmem_limit_bytes=16 * MIB),
    )(jnp.asarray(degree_gather_matrix()), recv, inverse)


def exchange(x):
    return lax.all_to_all(x, AXES, split_axis=0, concat_axis=0, tiled=True)


def on_device(grid_field, legendre, order_table, boundary_rows, inverse):
    core = (lax.axis_index("row") % 2).astype(jnp.int32).reshape(1)
    field = exchange(pack(grid_field, core))
    right_side = exchange(analysis(order_table, boundary_rows, field, legendre))
    return solve(right_side, inverse)


def solution(mesh):
    return jax.shard_map(
        on_device,
        mesh=mesh,
        in_specs=(
            P(None, "ma", "row"),
            P(("ma", "row"), None, None),
            P(("ma", "row")),
            P(),
            P(("ma", "row"), None, None),
        ),
        out_specs=P(("ma", "row"), None, None),
        check_vma=False,
    )
```

```python
import jax
import jax.numpy as jnp
import ml_dtypes
import numpy as np
from jax import lax
from jax.experimental import pallas as pl
from jax.experimental.pallas import tpu as pltpu
from jax.sharding import PartitionSpec as P

AXES = ("ma", "row")
NR = 128
COLS = 4 * NR
LAT_CHUNKS = (16, 24, 8)
LAT_PITCH = 24
ROW_BLOCK = 256
SRC_STEP = 128
SRC_PERM = 16
MIB = 1024 * 1024


def dot_nt(a, b):
    return lax.dot_general(a, b, (((1,), (1,)), ((), ())), preferred_element_type=jnp.float32)


def dot(a, b):
    return jnp.dot(a, b, preferred_element_type=jnp.float32)


def chebyshev_matrices():
    k = np.arange(NR, dtype=np.float64)[:, None]
    j = np.arange(NR, dtype=np.float64)[None, :]
    table = np.cos(np.pi * k * (j + 0.5) / NR) * np.sqrt(2.0 / NR)
    table[0] = np.sqrt(1.0 / NR)
    full = np.zeros((COLS, COLS), np.float64)
    for p in range(2):
        for q in range(2):
            full[2 * q + p :: 4, 256 * p + 128 * q : 256 * p + 128 * q + 128] = table.T
    full = full.astype(np.float32)
    swapped = full.reshape(4, 2, 64, COLS)[:, ::-1].reshape(COLS, COLS)
    full = np.stack([full, swapped])
    high = full.astype(ml_dtypes.bfloat16)
    low = (full - high.astype(np.float32)).astype(ml_dtypes.bfloat16)
    return high, low


def degree_gather_matrix():
    m = np.zeros((16 * SRC_PERM, 16 * SRC_PERM), np.float32)
    for p in range(2):
        for s in range(SRC_PERM):
            for h in range(2):
                for i in range(4):
                    m[((i * SRC_PERM + s) * 2 + h) * 2 + p, ((p * SRC_PERM + s) * 2 + h) * 4 + i] = 1.0
    return m.astype(ml_dtypes.bfloat16)


def pack_body(core_ref, x_hbm, o_hbm, x_ref, f_ref, o_ref, in_sem, out_sem):
    starts = [sum(LAT_CHUNKS[:i]) for i in range(len(LAT_CHUNKS))]
    parts = [pl.ds(first, size) for first, size in zip(starts, LAT_CHUNKS)]

    def fetch(i):
        return pltpu.make_async_copy(x_hbm.at[parts[i]], x_ref.at[parts[i]], in_sem.at[i])

    def flush(i):
        return pltpu.make_async_copy(o_ref.at[:, parts[i], :], o_hbm.at[:, parts[i], :], out_sem.at[i])

    for i in range(len(parts)):
        fetch(i).start()
    source = lax.broadcasted_iota(jnp.int32, (256, 256), 0)
    target = lax.broadcasted_iota(jnp.int32, (256, 256), 1)
    first = source == 2 * (target % 128) + target // 128
    second = source == 2 * (target % 128) + 1 - target // 128
    unzip = jnp.where(core_ref[0] == 0, first.astype(jnp.float32), second.astype(jnp.float32)).astype(jnp.bfloat16)
    for i, (start, size) in enumerate(zip(starts, LAT_CHUNKS)):
        lat = slice(start, start + size)
        fetch(i).wait()
        for g in range(2):
            x = x_ref[lat, :, g * 256 : (g + 1) * 256].reshape(size * 64, 256)
            y = dot(x, unzip).astype(jnp.bfloat16)
            for t in range(size):
                rows = slice(t * 64, (t + 1) * 64)
                b = jnp.concatenate([y[rows, :128], y[rows, 128:]], axis=0)
                f_ref[i, pl.ds(g * 128 * LAT_PITCH + t, 128, stride=LAT_PITCH), :] = b.T.astype(jnp.float32)
        o_ref[:, lat, :] = f_ref[i].reshape(256, LAT_PITCH, 128)[:, :size].astype(jnp.bfloat16)
        flush(i).start()
    for i in range(len(parts)):
        flush(i).wait()


def pack(grid_field, core):
    x = jnp.transpose(grid_field, (1, 2, 0))
    lat = x.shape[0]
    chunks = len(LAT_CHUNKS)
    return pl.pallas_call(
        pack_body,
        name="pack",
        in_specs=[pl.BlockSpec(memory_space=pltpu.SMEM), pl.BlockSpec(memory_space=pltpu.HBM)],
        out_specs=pl.BlockSpec(memory_space=pltpu.HBM),
        out_shape=jax.ShapeDtypeStruct((256, lat, 128), jnp.bfloat16),
        scratch_shapes=[
            pltpu.VMEM(x.shape, jnp.bfloat16),
            pltpu.VMEM((chunks, 256 * LAT_PITCH, 128), jnp.float32),
            pltpu.VMEM((256, lat, 128), jnp.bfloat16),
            pltpu.SemaphoreType.DMA((chunks,)),
            pltpu.SemaphoreType.DMA((chunks,)),
        ],
        compiler_params=pltpu.CompilerParams(vmem_limit_bytes=58 * MIB),
    )(core, x)


def analysis_body(order_ref, boundary_ref, recv_ref, leg_ref, chi_ref, clo_ref, o_ref, f_ref):
    column = lax.broadcasted_iota(jnp.int32, (1, COLS), 1)
    mode, second = column % NR, (column // NR) % 2 == 1
    keep = jnp.ones((1, COLS), jnp.float32)
    for e in range(2):
        keep = jnp.where(mode == jnp.where(second, boundary_ref[1, e], boundary_ref[0, e]), 0.0, keep)
    lane = lax.broadcasted_iota(jnp.int32, (48, 128), 1)
    for a in range(32):
        for y in range(4):
            u = recv_ref[a * 8 + 2 * y]
            v = recv_ref[a * 8 + 2 * y + 1]
            f_ref[0, a * 48 : (a + 1) * 48, y * 128 : (y + 1) * 128] = jnp.where(lane < 64, u, v)
            f_ref[1, a * 48 : (a + 1) * 48, y * 128 : (y + 1) * 128] = jnp.where(lane < 64, v, u)

    iota = lax.broadcasted_iota(jnp.int32, (ROW_BLOCK, COLS), 0)
    sub = lax.broadcasted_iota(jnp.int32, (ROW_BLOCK // 8, 8, COLS), 1)
    step = ROW_BLOCK // 4

    def spectrum(h, block, masked):
        first = block * ROW_BLOCK
        if not isinstance(block, int):
            first = pl.multiple_of(first, ROW_BLOCK)
        s = dot(leg_ref[h, pl.ds(first, ROW_BLOCK)], f_ref[h])
        return jnp.where(iota + first >= order_ref[h], s, 0.0) if masked else s

    def transform(h, s):
        hi = s.astype(jnp.bfloat16)
        lo = (s - hi.astype(jnp.float32)).astype(jnp.bfloat16)
        c = dot(hi, clo_ref[h]) + dot(lo, chi_ref[h]) + dot(hi, chi_ref[h])
        return (c * keep).reshape(ROW_BLOCK // 8, 8, COLS)

    def store(block, a, b):
        even = jnp.where(sub < 4, a, 0.0 if b is None else pltpu.roll(b, 4, 1))
        odd = jnp.where(sub < 4, pltpu.roll(a, 4, 1), 0.0 if b is None else b)
        both = jnp.stack([even, odd], axis=1).reshape(step, 8, COLS)
        o_ref[block * step : (block + 1) * step] = both.astype(jnp.bfloat16)

    low_order = order_ref[0] < ROW_BLOCK
    h = jnp.where(low_order, 0, 1)
    s0 = spectrum(h, jnp.where(low_order, 0, 2), True)
    s1 = spectrum(0, 1, True)
    either = transform(h, s0)
    s2 = spectrum(0, 2, False)
    store(0, jnp.where(low_order, either, 0.0), None)
    c1 = transform(0, s1)
    s3 = spectrum(0, 3, False)
    store(1, c1, None)
    c2 = transform(0, s2)
    s4 = spectrum(1, 3, True)
    store(2, c2, jnp.where(low_order, 0.0, either))
    c3 = transform(0, s3)
    c4 = transform(1, s4)
    store(3, c3, c4)


def analysis(order_table, boundary_rows, recv, legendre):
    chi, clo = chebyshev_matrices()
    smem = pl.BlockSpec(memory_space=pltpu.SMEM)
    vmem = pl.BlockSpec(memory_space=pltpu.VMEM)
    return pl.pallas_call(
        analysis_body,
        name="analysis",
        in_specs=[smem, smem, vmem, vmem, vmem, vmem],
        out_specs=vmem,
        out_shape=jax.ShapeDtypeStruct((256, 8, COLS), jnp.bfloat16),
        scratch_shapes=[pltpu.VMEM((2, 1536, COLS), jnp.bfloat16)],
        compiler_params=pltpu.CompilerParams(vmem_limit_bytes=24 * MIB),
    )(order_table, boundary_rows, recv, legendre, jnp.asarray(chi), jnp.asarray(clo))


def solve_body(gather_ref, recv_ref, inverse_ref, o_hbm, o_ref, sem):
    chunks = 256 // SRC_STEP
    wide = 4 * SRC_STEP

    def flush(c, i):
        part = pl.ds(c * wide, wide)
        return pltpu.make_async_copy(o_ref.at[i, :, part], o_hbm.at[i, :, part], sem.at[c, i])

    per = 4 * SRC_PERM
    for c in range(chunks):
        parts = []
        for first in range(c * SRC_STEP, (c + 1) * SRC_STEP, SRC_PERM):
            block = recv_ref[first : first + SRC_PERM].reshape(SRC_PERM * 8, COLS)
            rows = jnp.concatenate([block[:, :256], block[:, 256:]], axis=0)
            parts.append(dot(gather_ref[...], rows).astype(jnp.bfloat16))
        for i in range(4):
            r = jnp.concatenate([part[i * per : (i + 1) * per] for part in parts], axis=0)
            o_ref[i, :, c * wide : (c + 1) * wide] = dot_nt(inverse_ref[i], r).astype(jnp.bfloat16)
            flush(c, i).start()
    for c in range(chunks):
        for i in range(4):
            flush(c, i).wait()


def solve(recv, inverse):
    vmem = pl.BlockSpec(memory_space=pltpu.VMEM)
    return pl.pallas_call(
        solve_body,
        name="solve",
        in_specs=[vmem, vmem, vmem],
        out_specs=pl.BlockSpec(memory_space=pltpu.HBM),
        out_shape=jax.ShapeDtypeStruct((4, 256, 1024), jnp.bfloat16),
        scratch_shapes=[
            pltpu.VMEM((4, 256, 1024), jnp.bfloat16),
            pltpu.SemaphoreType.DMA((256 // SRC_STEP, 4)),
        ],
        compiler_params=pltpu.CompilerParams(vmem_limit_bytes=16 * MIB),
    )(jnp.asarray(degree_gather_matrix()), recv, inverse)


def exchange(x):
    return lax.all_to_all(x, AXES, split_axis=0, concat_axis=0, tiled=True)


def on_device(grid_field, legendre, order_table, boundary_rows, inverse):
    core = (lax.axis_index("row") % 2).astype(jnp.int32).reshape(1)
    field = exchange(pack(grid_field, core))
    right_side = exchange(analysis(order_table, boundary_rows, field, legendre))
    return solve(right_side, inverse)


def solution(mesh):
    return jax.shard_map(
        on_device,
        mesh=mesh,
        in_specs=(
            P(None, "ma", "row"),
            P(("ma", "row"), None, None),
            P(("ma", "row")),
            P(),
            P(("ma", "row"), None, None),
        ),
        out_specs=P(("ma", "row"), None, None),
        check_vma=False,
    )
```
